256 devices in a mesh: seq: 32 (over y, x, core), tp: 8 (over z).
Axes of the slice: x: 4, y: 4, z: 8, core: 2. Of those that a mesh axis runs over, the one named last changes fastest.
Arguments:
- hidden_in: bfloat16 [4096, 4096], P('seq', 'tp'), may hold values from -3 to 3
- norm_gain: bfloat16 [4096], replicated, may hold values from 0.099609375 to 1.8984375
- w_query: bfloat16 [4096, 4096], P(None, 'tp'), may hold values from -0.09375 to 0.09375
- w_keyval: bfloat16 [4096, 2048], P(None, 'tp'), may hold values from -0.09375 to 0.09375
- w_out: bfloat16 [4096, 4096], P('tp'), may hold values from -0.375 to 0.375
- kv_cache: bfloat16 [96, 128, 2048], P('seq', None, 'tp'), may hold values from -80 to 80, as said below
- cached_lengths: int32 [2], replicated, may hold values from 256 to 4096, as said below
- block_table: int32 [96], replicated, may hold values from 0 to 95, each once
Outputs:
- hidden_out: bfloat16 [4096, 4096], P('seq', 'tp')
- kv_out: bfloat16 [96, 128, 2048], P('seq', None, 'tp')
The draws below stay inside these ranges and needn't reach their ends.
Inputs may be any that keep to these rules, and one draw needn't show every extreme that they name: `cached_lengths`: one request, picked by the seed, has exactly 4096 cached rows; each other has 256 to 512. `block_table`: entry r * 48 + j is the slot of rows j * 128 to j * 128 + 127 of request r; each slot once. `kv_cache`: rows past a request's cached length hold arbitrary values.
All inputs are finite; a program needn't handle non-finite values.
Results may differ from the reference program's by a relative error of at most 0.015.
The reference program's roundings to bfloat16 on the way count: a program that leaves them out, or rounds other values in their place, can miss the bound.
Values may be sent and summed in bfloat16 or wider, within the bound.
No kernel may reach another device: no remote copies, remote signals or barrier semaphores. Data moves between devices by JAX's collectives and lax.ppermute only.
A program may use at most 128 MiB of HBM per device.

```python
import math
import jax
import jax.numpy as jnp
from jax import lax

D = 4096
H = 32
KVH = 8
HD = 128
BLOCK = 128
R = 2
TOKENS = 4096
SPAN = 2048
MAXLEN = 4096
MAXBLK = 48
SLOTS = 96


def draw_kv_cache(key, part):
    base_key = jax.random.fold_in(key, 0)
    full_shape = (SLOTS, BLOCK, KVH * 2 * HD)
    values = jnp.clip(jax.random.normal(base_key, full_shape, jnp.float32), -6.0, 6.0)
    return values.astype(jnp.bfloat16)


def draw_cached_lengths(key, part):
    order_key, short_key = jax.random.split(key)
    ranking = jax.random.permutation(order_key, R)
    shorter = jax.random.randint(short_key, (R,), MAXLEN // 16, MAXLEN // 8 + 1)
    return jnp.where(ranking == 0, MAXLEN, shorter).astype(jnp.int32)


def block_scale(rng, extent, cuts, smallest, largest):
    factor_of, own = 1.0, jax.random.fold_in(rng, 6)
    for position, shards_of in cuts:
        draws = jnp.exp(jax.random.uniform(jax.random.fold_in(own, position), (shards_of,), jnp.float32, smallest / len(cuts), largest / len(cuts)))
        factor_of = factor_of * jnp.repeat(draws, extent[position] // shards_of).reshape([-1 if axis == position else 1 for axis in range(len(extent))])
    return factor_of


def bell_draw(own_key, shape, spread, bound, pieces=(), kind=jnp.bfloat16):
    values = spread * jax.random.normal(own_key, shape, jnp.float32)
    if pieces:
        values = values * block_scale(own_key, shape, pieces, -0.22, 0.18)
    return jnp.clip(values, -bound, bound).astype(kind)


def setup_inputs(seed: int = 0) -> dict:
    splits = jax.random.split(jax.random.key(seed), 9)
    hidden_in = bell_draw(splits[0], (TOKENS, D), 0.5, 3.0, ((0, 32), (1, 8)))
    norm_gain = jnp.clip(1.0 + 0.18 * jax.random.normal(splits[1], (D,), jnp.float32), 0.099609375, 1.8984375).astype(jnp.bfloat16)
    w_query = bell_draw(splits[2], (D, H * HD), D ** -0.5, 0.09375, ((1, 8),))
    w_keyval = bell_draw(splits[3], (D, KVH * 2 * HD), D ** -0.5, 0.09375, ((1, 8),))
    w_out = bell_draw(splits[4], (H * HD, D), ((H * HD) // 16) ** -0.5, 0.375, ((0, 8),))
    kv_cache = draw_kv_cache(jax.random.fold_in(splits[8], 71), 0)
    cached_lengths = draw_cached_lengths(jax.random.fold_in(splits[8], 71), 0)
    block_table = jax.random.permutation(splits[7], SLOTS).astype(jnp.int32)
    return {"hidden_in": hidden_in, "norm_gain": norm_gain, "w_query": w_query, "w_keyval": w_keyval, "w_out": w_out, "kv_cache": kv_cache, "cached_lengths": cached_lengths, "block_table": block_table}


EPSILON = 1e-05
ROPE_BASE = 500000.0
MASKED = -1e+30

def rotate(values, positions):
    full_width = values.shape[-1]
    half_width = full_width // 2
    frequency = ROPE_BASE ** (-2.0 * jnp.arange(half_width, dtype=jnp.float32) / full_width)
    angles = positions.astype(jnp.float32)[:, None] * frequency[None, :]
    cosine = jnp.cos(angles)[:, None, :]
    sines = jnp.sin(angles)[:, None, :]
    first_half = values[..., :half_width]
    second_half = values[..., half_width:]
    return jnp.concatenate([first_half * cosine - second_half * sines, second_half * cosine + first_half * sines], axis=-1)

def attend_request(queries, keys, values, key_position, key_live, query_position):
    block_rows = min(128, SPAN)
    block_count = SPAN // block_rows
    grouped = queries.reshape(block_count, block_rows, KVH, H // KVH, HD)
    grouped_position = query_position.reshape(block_count, block_rows)
    keys_wide = keys.astype(jnp.float32)
    values_wide = values.astype(jnp.float32)
    score_scale = 1.0 / math.sqrt(HD)

    def one_block(operands):
        query_block, position_block = operands
        scores = jnp.einsum('nhgd,khd->nhgk', query_block.astype(jnp.float32), keys_wide) * score_scale
        visible = key_live[None, :] & (key_position[None, :] <= position_block[:, None])
        keep_mask = visible[:, None, None, :]
        scores = jnp.where(keep_mask, scores, MASKED)
        row_max = lax.optimization_barrier(jnp.max(scores, axis=-1, keepdims=True))
        weights = jnp.where(keep_mask, jnp.exp(scores - row_max), 0.0)
        row_sum = lax.optimization_barrier(jnp.sum(weights, axis=-1))
        probs = lax.optimization_barrier(weights.astype(jnp.bfloat16)).astype(jnp.float32)
        mixed = jnp.einsum('nhgk,khd->nhgd', probs, values_wide)
        return (mixed / row_sum[..., None]).astype(jnp.bfloat16)
    outputs = lax.map(one_block, (grouped, grouped_position))
    return outputs.reshape(SPAN, H * HD)

def reference(hidden_in, norm_gain, w_query, w_keyval, w_out, kv_cache, cached_lengths, block_table):
    widened = hidden_in.astype(jnp.float32)
    normed = (widened * lax.rsqrt(lax.optimization_barrier(jnp.mean(widened * widened, axis=1, keepdims=True)) + EPSILON) * norm_gain.astype(jnp.float32)).astype(jnp.bfloat16)
    token_ids = jnp.arange(TOKENS, dtype=jnp.int32)
    request_ids = token_ids // SPAN
    positions = (cached_lengths[request_ids] + token_ids % SPAN).astype(jnp.int32)
    projected = jnp.dot(normed, w_query, preferred_element_type=jnp.float32).reshape(TOKENS, H, HD)
    queries = rotate(projected, positions).astype(jnp.bfloat16)
    key_value = jnp.dot(normed, w_keyval, preferred_element_type=jnp.float32).reshape(TOKENS, KVH, 2, HD)
    fresh_rows = jnp.stack([rotate(key_value[:, :, 0], positions), key_value[:, :, 1]], axis=2).astype(jnp.bfloat16)
    slot_index = block_table[request_ids * MAXBLK + positions // BLOCK]
    kv_out = kv_cache.at[slot_index, positions % BLOCK].set(fresh_rows.reshape(TOKENS, KVH * 2 * HD))
    cache_blocks = MAXLEN // BLOCK
    attended = []
    for request in range(R):
        page_rows = block_table[request * MAXBLK:request * MAXBLK + cache_blocks]
        stored = kv_cache[page_rows].reshape(MAXLEN, KVH, 2, HD)
        new_part = fresh_rows[request * SPAN:(request + 1) * SPAN]
        all_rows = jnp.concatenate([stored, new_part], axis=0)
        length = cached_lengths[request]
        stored_position = jnp.arange(MAXLEN, dtype=jnp.int32)
        query_position = positions[request * SPAN:(request + 1) * SPAN]
        key_position = jnp.concatenate([stored_position, query_position])
        key_live = jnp.concatenate([stored_position < length, jnp.ones((SPAN,), dtype=jnp.bool_)])
        request_queries = queries[request * SPAN:(request + 1) * SPAN].reshape(SPAN, KVH, H // KVH, HD)
        attended.append(attend_request(request_queries, all_rows[:, :, 0], all_rows[:, :, 1], key_position, key_live, query_position))
    attended = jnp.concatenate(attended, axis=0)
    hidden_out = (widened + jnp.dot(attended, w_out, preferred_element_type=jnp.float32)).astype(jnp.bfloat16)
    return (hidden_out, kv_out)
```

```python
import functools
import math

import jax
import jax.numpy as jnp
from jax import lax
from jax.experimental import pallas as pl
from jax.experimental.pallas import tpu as pltpu
from jax.sharding import PartitionSpec as P

HD = 128
BLOCK = 128
NEW = 16
MAXBLK = 48
CACHED = 32
EPSILON = 1e-05
ROPE_BASE = 500000.0
MASKED = -1e30
SCALE = 1.0 / math.sqrt(HD)
SCALE2 = SCALE * 1.4426950408889634
LEN_AT, S_AT, Z_AT = 96, 98, 99


ANY = pl.BlockSpec(memory_space=pl.ANY)
VM = pl.BlockSpec(memory_space=pltpu.VMEM)


def coords(s):
    return s % 2, (s // 2) % 4, s // 8


def seq_move(value, target):
    pairs = []
    for s in range(32):
        c, x, y = coords(s)
        c2, x2, y2 = target(c, x, y)
        pairs.append((s, ((y2 % 4) * 4 + x2 % 4) * 2 + c2))
    return lax.ppermute(value, "seq", pairs)


def move_x(value, k):
    return seq_move(value, lambda c, x, y: (c, x + k, y))


def move_y(value, k):
    return seq_move(value, lambda c, x, y: (c, x, y + k))


def pair_y(value):
    return seq_move(value, lambda c, x, y: (c, x, y ^ 1))


def other_core(value):
    return seq_move(value, lambda c, x, y: (1 - c, x, y))


def first_axis(value, k):
    return seq_move(value, lambda c, x, y: (c, x + k, y) if c == 0 else (c, x, y + k))


def second_axis(value, k):
    return seq_move(value, lambda c, x, y: (c, x, y + k) if c == 0 else (c, x + k, y))


def move_z(value, k):
    return lax.ppermute(value, "tp", [(i, (i + k) % 8) for i in range(8)])


def place(d):
    return d ^ (d >> 1)


def rotated(u, cosine, sine):
    return u * cosine + pltpu.roll(u, HD // 2, 1) * sine


def project_kernel(
    scal, x0, f1, b1, f2, b2, f3, b3, f4, b4, gain, cosine, sine, wq, wkv, q_out, n_out, wq_v, wkv_v, sem
):
    z = scal[Z_AT]
    shifts = (0, 1, 7, 2, 6, 3, 5, 4)

    def copies(i):
        src = (z + 8 - shifts[i]) % 8
        rows = pl.ds(pl.multiple_of(src * 512, 512), 512)
        return (
            pltpu.make_async_copy(wq.at[rows], wq_v.at[i], sem.at[i]),
            pltpu.make_async_copy(wkv.at[rows], wkv_v.at[i], sem.at[8 + i]),
        )

    for i in range(8):
        for copy in copies(i):
            copy.start()
    last = jnp.concatenate([f4[...], b4[...]], axis=0)
    chunks = [r[...].astype(jnp.float32) for r in (x0, f1, b1, f2, b2, f3, b3)]
    chunks.append(last.astype(jnp.float32))
    squares = chunks[0] * chunks[0]
    for chunk in chunks[1:]:
        squares = squares + chunk * chunk
    mean = jnp.sum(squares, axis=1, keepdims=True) * (1.0 / 4096.0)
    inverse = lax.rsqrt(mean + EPSILON)
    acc_q = jnp.zeros((128, 512), jnp.float32)
    acc_n = jnp.zeros((128, 256), jnp.float32)
    for i in range(8):
        src = (z + 8 - shifts[i]) % 8
        normed = (chunks[i] * inverse * gain[pl.ds(src, 1), 0, :]).astype(jnp.bfloat16)
        for copy in copies(i):
            copy.wait()
        acc_q = acc_q + jnp.dot(normed, wq_v[i], preferred_element_type=jnp.float32)
        acc_n = acc_n + jnp.dot(normed, wkv_v[i], preferred_element_type=jnp.float32)
    cos = cosine[...]
    sin = sine[...]
    for h in range(4):
        part = rotated(acc_q[:, h * HD : (h + 1) * HD], cos, sin)
        q_out[h * 128 : (h + 1) * 128, :] = part.astype(jnp.bfloat16)
    n_out[:, :HD] = rotated(acc_n[:, :HD], cos, sin).astype(jnp.bfloat16)
    n_out[:, HD:] = acc_n[:, HD:].astype(jnp.bfloat16)


def project(scal, chunks, gain, cosine, sine, w_query, w_keyval):
    return pl.pallas_call(
        project_kernel,
        out_shape=(
            jax.ShapeDtypeStruct((512, HD), jnp.bfloat16),
            jax.ShapeDtypeStruct((128, 256), jnp.bfloat16),
        ),
        grid_spec=pltpu.PrefetchScalarGridSpec(
            num_scalar_prefetch=1,
            grid=(),
            in_specs=[VM] * 12 + [ANY, ANY],
            out_specs=(VM, VM),
            scratch_shapes=[
                pltpu.VMEM((8, 512, 512), jnp.bfloat16),
                pltpu.VMEM((8, 512, 256), jnp.bfloat16),
                pltpu.SemaphoreType.DMA((16,)),
            ],
        ),
        cost_estimate=pl.CostEstimate(
            flops=2 * 128 * 4096 * 768, bytes_accessed=8 << 20, transcendentals=0
        ),
        name="project",
    )(scal, *chunks, gain, cosine, sine, w_query, w_keyval)


def attend_kernel(
    scal, q, s0, r0, l0, o0, p0, s1, r1, l1, o1, p1, fa, fb, out, kv, m_ref, l_ref, acc, sem
):
    me = scal[S_AT]
    core, my_x, my_y = me % 2, (me // 2) % 4, me // 8
    request = me // NEW
    mine = me % NEW
    length = scal[LEN_AT + request]
    cached = (length + BLOCK - 1) // BLOCK
    own_set = (s0, r0, l0, o0, p0)
    other_set = (s1, r1, l1, o1, p1)

    @pl.loop(0, cached)
    def _(j):
        slot = scal[request * MAXBLK + j]
        device = slot // 3
        at = slot - 3 * device
        c, x, y = device % 2, (device // 2) % 4, device // 8
        dx, dy = (my_x - x) & 3, (my_y - y) & 3
        near = jnp.where(c == 0, dx, dy)
        far = jnp.where(c == 0, dy, dx)
        index = 3 * place(near) + at
        same = c == core

        def fetch(ref, i):
            pltpu.make_async_copy(ref.at[i], kv.at[j], sem.at[j]).start()

        for which, refs in ((same, own_set), (jnp.logical_not(same), other_set)):

            @pl.when(which)
            def _(refs=refs):
                for d in (0, 1, 3):
                    ref = refs[{0: 0, 1: 1, 3: 2}[d]]

                    @pl.when(far == d)
                    def _(ref=ref):
                        fetch(ref, index)

                @pl.when((far == 2) & (index < 6))
                def _():
                    fetch(refs[3], jnp.minimum(index, 5))

                @pl.when((far == 2) & (index >= 6))
                def _():
                    fetch(refs[4], jnp.maximum(index - 6, 0))

    @pl.loop(0, mine + 1)
    def _(k):
        device = request * NEW + k
        c, x, y = device % 2, (device // 2) % 4, device // 8
        index = 2 * place((my_x - x) & 3) + ((my_y ^ y) & 1)

        @pl.when(c == core)
        def _():
            pltpu.make_async_copy(fa.at[index], kv.at[CACHED + k], sem.at[CACHED + k]).start()

        @pl.when(c != core)
        def _():
            pltpu.make_async_copy(fb.at[index], kv.at[CACHED + k], sem.at[CACHED + k]).start()

    m_ref[...] = jnp.full_like(m_ref, MASKED)
    l_ref[...] = jnp.zeros_like(l_ref)
    acc[...] = jnp.zeros_like(acc)

    def step(first, count, keep=None):
        for b in range(count):
            pltpu.make_async_copy(fa.at[0], kv.at[first + b], sem.at[first + b]).wait()
        pages = kv[pl.ds(first, count)].reshape(count * BLOCK, 256)
        keys, values = pages[:, :HD], pages[:, HD:]
        for h in range(4):
            rows = slice(h * 128, (h + 1) * 128)
            scores = lax.dot_general(
                q[rows, :], keys, (((1,), (1,)), ((), ())), preferred_element_type=jnp.float32
            )
            if keep is not None:
                scores = jnp.where(keep, scores, MASKED)
            old = m_ref[rows, :]
            new = jnp.maximum(old, jnp.max(scores, axis=1, keepdims=True))
            weights = jnp.exp2((scores - new[:, :1]) * SCALE2)
            if keep is not None:
                weights = jnp.where(keep, weights, 0.0)
            factor = jnp.exp2((old - new) * SCALE2)
            lanes = weights[:, :128]
            for b in range(1, count):
                lanes = lanes + weights[:, b * 128 : (b + 1) * 128]
            m_ref[rows, :] = new
            l_ref[rows, :] = l_ref[rows, :] * factor + lanes
            acc[rows, :] = acc[rows, :] * factor + jnp.dot(
                weights.astype(jnp.bfloat16), values, preferred_element_type=jnp.float32
            )

    column = lax.broadcasted_iota(jnp.int32, (128, 128), 1)
    row = lax.broadcasted_iota(jnp.int32, (128, 128), 0)
    whole = length // 512

    @pl.loop(0, whole)
    def _(i):
        step(i * 4, 4)

    @pl.loop(whole * 4, cached)
    def _(j):
        step(j, 1, column < length - j * BLOCK)

    @pl.loop(0, mine // 4)
    def _(i):
        step(CACHED + i * 4, 4)

    @pl.loop((mine // 4) * 4, mine)
    def _(k):
        step(CACHED + k, 1)

    step(CACHED + mine, 1, column <= row)
    for h in range(4):
        rows = slice(h * 128, (h + 1) * 128)
        total = jnp.sum(l_ref[rows, :], axis=1, keepdims=True)
        out[:, h * HD : (h + 1) * HD] = (acc[rows, :] / total).astype(jnp.bfloat16)


def attend(scal, q, own_set, other_set, fresh_own, fresh_other):
    return pl.pallas_call(
        attend_kernel,
        out_shape=jax.ShapeDtypeStruct((128, 512), jnp.bfloat16),
        grid_spec=pltpu.PrefetchScalarGridSpec(
            num_scalar_prefetch=1,
            grid=(),
            in_specs=[VM] + [ANY] * 12,
            out_specs=VM,
            scratch_shapes=[
                pltpu.VMEM((CACHED + NEW, BLOCK, 256), jnp.bfloat16),
                pltpu.VMEM((512, 128), jnp.float32),
                pltpu.VMEM((512, 128), jnp.float32),
                pltpu.VMEM((512, 128), jnp.float32),
                pltpu.SemaphoreType.DMA((CACHED + NEW,)),
            ],
        ),
        cost_estimate=pl.CostEstimate(
            flops=4 * 512 * 128 * 6144, bytes_accessed=4 << 20, transcendentals=512 * 6144
        ),
        name="attend",
    )(scal, q, *own_set, *other_set, fresh_own, fresh_other)


def output_kernel(shifts, scal, attended, w_out, *rest):
    outs, w_v, sem = rest[: len(shifts)], rest[-2], rest[-1]
    z = scal[Z_AT]

    def copy(i):
        to = (z + shifts[i]) % 8
        columns = pl.ds(pl.multiple_of(to * 512, 512), 512)
        return pltpu.make_async_copy(w_out.at[:, columns], w_v.at[i], sem.at[i])

    for i in range(len(shifts)):
        copy(i).start()
    rows = attended[...]
    for i in range(len(shifts)):
        copy(i).wait()
        outs[i][...] = jnp.dot(rows, w_v[i], preferred_element_type=jnp.float32).astype(
            outs[i].dtype
        )


def output_terms(scal, attended, w_out, shifts):
    n = len(shifts)
    return pl.pallas_call(
        functools.partial(output_kernel, shifts),
        out_shape=[
            jax.ShapeDtypeStruct((128, 512), jnp.float32 if k == 0 else jnp.bfloat16)
            for k in shifts
        ],
        grid_spec=pltpu.PrefetchScalarGridSpec(
            num_scalar_prefetch=1,
            grid=(),
            in_specs=[VM, ANY],
            out_specs=[VM] * n,
            scratch_shapes=[
                pltpu.VMEM((n, 512, 512), jnp.bfloat16),
                pltpu.SemaphoreType.DMA((n,)),
            ],
        ),
        cost_estimate=pl.CostEstimate(
            flops=2 * 128 * 512 * 512 * n, bytes_accessed=n << 19, transcendentals=0
        ),
        name="output_terms",
    )(scal, attended, w_out)


def write_kernel(scal, cache, fa, fb, ga, gb, out, buf, sem):
    me = scal[S_AT]
    core, my_x, my_y = me % 2, (me // 2) % 4, me // 8
    base = me * 3
    found = [jnp.int32(0)] * 3
    for entry in range(96):
        slot = scal[entry] - base
        for i in range(3):
            found[i] = jnp.where(slot == i, entry, found[i])
    starts = []
    for i in range(3):
        request = found[i] // MAXBLK
        start = (found[i] % MAXBLK) * BLOCK - scal[LEN_AT + request]
        block = (start + 64 * BLOCK) // BLOCK - 64
        starts.append((start, block))
        for half in range(2):
            k = block + half
            inside = (k >= 0) & (k < NEW)
            safe = jnp.clip(k, 0, NEW - 1)
            device = request * NEW + safe
            c, x, y = device % 2, (device // 2) % 4, device // 8
            index = 2 * place((my_x - x) & 3) + ((my_y ^ y) & 1)
            near = (y // 2) == (my_y // 2)
            same = c == core
            for cond, ref in (
                (near & same, fa),
                (near & jnp.logical_not(same), fb),
                (jnp.logical_not(near) & same, ga),
                (jnp.logical_not(near) & jnp.logical_not(same), gb),
            ):

                @pl.when(cond & inside)
                def _(ref=ref, index=index, n=2 * i + half):
                    pltpu.make_async_copy(ref.at[index], buf.at[n], sem.at[n]).start()

            @pl.when(jnp.logical_not(inside))
            def _(n=2 * i + half):
                buf[n] = jnp.zeros((BLOCK, 256), jnp.bfloat16)

    row = lax.broadcasted_iota(jnp.int32, (BLOCK, BLOCK), 0)
    column = lax.broadcasted_iota(jnp.int32, (BLOCK, BLOCK), 1)
    tall = lax.broadcasted_iota(jnp.int32, (BLOCK, 256), 0)
    for i in range(3):
        start, block = starts[i]
        offset = start - block * BLOCK
        for half in range(2):
            k = block + half

            @pl.when((k >= 0) & (k < NEW))
            def _(n=2 * i + half):
                pltpu.make_async_copy(fa.at[0], buf.at[n], sem.at[n]).wait()

        low = jnp.where(column == row + offset, 1.0, 0.0).astype(jnp.bfloat16)
        high = jnp.where(column + BLOCK == row + offset, 1.0, 0.0).astype(jnp.bfloat16)
        rows = jnp.dot(low, buf[2 * i], preferred_element_type=jnp.float32)
        rows = rows + jnp.dot(high, buf[2 * i + 1], preferred_element_type=jnp.float32)
        token = tall + start
        written = (token >= 0) & (token < NEW * BLOCK)
        out[i] = jnp.where(written, rows, cache[i].astype(jnp.float32)).astype(jnp.bfloat16)


def write_rows(scal, kv_cache, *fresh):
    return pl.pallas_call(
        write_kernel,
        out_shape=jax.ShapeDtypeStruct(kv_cache.shape, jnp.bfloat16),
        grid_spec=pltpu.PrefetchScalarGridSpec(
            num_scalar_prefetch=1,
            grid=(),
            in_specs=[VM] + [ANY] * 4,
            out_specs=VM,
            scratch_shapes=[
                pltpu.VMEM((6, BLOCK, 256), jnp.bfloat16),
                pltpu.SemaphoreType.DMA((6,)),
            ],
        ),
        cost_estimate=pl.CostEstimate(
            flops=2 * 3 * 128 * 256 * 256, bytes_accessed=1 << 20, transcendentals=0
        ),
        name="write_rows",
    )(scal, kv_cache, *fresh)


def shards(hidden_in, norm_gain, w_query, w_keyval, w_out, kv_cache, cached_lengths, block_table):
    s = lax.axis_index("seq")
    z = lax.axis_index("tp")
    scal = jnp.concatenate(
        [block_table, cached_lengths, jnp.stack([s, z]).astype(jnp.int32)]
    )
    request = s // NEW
    length = jnp.where(request == 0, cached_lengths[0], cached_lengths[1])
    position = length + (s % NEW) * BLOCK + jnp.arange(BLOCK, dtype=jnp.int32)
    frequency = ROPE_BASE ** (-2.0 * jnp.arange(HD // 2, dtype=jnp.float32) / HD)
    angles = position.astype(jnp.float32)[:, None] * frequency[None, :]
    cosine = jnp.cos(angles)
    sine = jnp.sin(angles)
    cosine = jnp.concatenate([cosine, cosine], axis=1)
    sine = jnp.concatenate([-sine, sine], axis=1)
    gain = norm_gain.astype(jnp.float32).reshape(8, 1, 512)

    up, down = [hidden_in], [hidden_in]
    for _ in range(3):
        up.append(move_z(up[-1], 1))
        down.append(move_z(down[-1], -1))
    up.append(move_z(up[3][:64], 1))
    down.append(move_z(down[3][64:], -1))
    chunks = [hidden_in] + [a for k in range(1, 5) for a in (up[k], down[k])]

    own = kv_cache.reshape(384, 256)
    near = jnp.concatenate(
        [
            own,
            first_axis(own, 1),
            first_axis(own, -1),
            first_axis(own[:192], 2),
            first_axis(own[192:], -2),
        ],
        axis=0,
    ).reshape(12, BLOCK, 256)
    own_set = [
        near,
        second_axis(near, 1),
        second_axis(near, -1),
        second_axis(near[:6], 2),
        second_axis(near[6:], -2),
    ]
    other_set = [other_core(a) for a in own_set]

    queries, fresh = project(scal, chunks, gain, cosine, sine, w_query, w_keyval)
    two = jnp.stack([fresh, pair_y(fresh)])
    fresh_own = jnp.concatenate(
        [two, move_x(two, 1), move_x(two, -1), move_x(two[:1], 2), move_x(two[1:], -2)], axis=0
    )
    fresh_other = other_core(fresh_own)
    attended = attend(scal, queries, own_set, other_set, fresh_own, fresh_other)

    far_own = move_y(fresh_own, 2)
    far_other = other_core(far_own)
    kv_out = write_rows(scal, kv_cache, fresh_own, fresh_other, far_own, far_other)

    (t4,) = output_terms(scal, attended, w_out, (4,))
    ahead, behind = move_z(t4[:64], 1), move_z(t4[64:], -1)
    t3, t5, t2, t6, t1, t7, t0 = output_terms(scal, attended, w_out, (3, 5, 2, 6, 1, 7, 0))

    def add(a, b):
        return (a.astype(jnp.float32) + b.astype(jnp.float32)).astype(jnp.bfloat16)

    ahead = jnp.concatenate([add(t3[:64], ahead), t3[64:]], axis=0)
    behind = jnp.concatenate([t5[:64], add(t5[64:], behind)], axis=0)
    ahead, behind = move_z(ahead, 1), move_z(behind, -1)
    ahead, behind = move_z(add(t2, ahead), 1), move_z(add(t6, behind), -1)
    ahead, behind = move_z(add(t1, ahead), 1), move_z(add(t7, behind), -1)
    total = t0 + ahead.astype(jnp.float32) + behind.astype(jnp.float32)
    hidden_out = (hidden_in.astype(jnp.float32) + total).astype(jnp.bfloat16)
    return hidden_out, kv_out


def solution(mesh):
    return jax.shard_map(
        shards,
        mesh=mesh,
        in_specs=(
            P("seq", "tp"),
            P(),
            P(None, "tp"),
            P(None, "tp"),
            P("tp", None),
            P("seq", None, "tp"),
            P(),
            P(),
        ),
        out_specs=(P("seq", "tp"), P("seq", None, "tp")),
        check_vma=False,
    )
```

```python
import functools
import math

import jax
import jax.numpy as jnp
import numpy as np
from jax import lax
from jax.experimental import pallas as pl
from jax.experimental.pallas import tpu as pltpu
from jax.sharding import PartitionSpec as P

HD = 128
BLOCK = 128
NEW = 16
MAXBLK = 48
CACHED = 32
EPSILON = 1e-05
ROPE_BASE = 500000.0
MASKED = -1e30
SCALE = 1.0 / math.sqrt(HD)
SCALE2 = SCALE * 1.4426950408889634
BT_AT, LEN_AT, S_AT, Z_AT = 96, 192, 194, 195
PROJECT_VMEM = 4 << 20
ATTEND_VMEM = 20 << 20
SMALL_VMEM = 4 << 20


ANY = pl.BlockSpec(memory_space=pl.ANY)
VM = pl.BlockSpec(memory_space=pltpu.VMEM)


def coords(s):
    return s % 2, (s // 2) % 4, s // 8


def seq_move(value, target):
    pairs = []
    for s in range(32):
        c, x, y = coords(s)
        c2, x2, y2 = target(c, x, y)
        pairs.append((s, ((y2 % 4) * 4 + x2 % 4) * 2 + c2))
    return lax.ppermute(value, "seq", pairs)


def move_x(value, k):
    return seq_move(value, lambda c, x, y: (c, x + k, y))


def move_y(value, k):
    return seq_move(value, lambda c, x, y: (c, x, y + k))


def pair_y(value):
    return seq_move(value, lambda c, x, y: (c, x, y ^ 1))


def other_core(value):
    return seq_move(value, lambda c, x, y: (1 - c, x, y))


def first_axis(value, k):
    return seq_move(value, lambda c, x, y: (c, x + k, y) if c == 0 else (c, x, y + k))


def second_axis(value, k):
    return seq_move(value, lambda c, x, y: (c, x, y + k) if c == 0 else (c, x + k, y))


def move_z(value, k):
    return lax.ppermute(value, "tp", [(i, (i + k) % 8) for i in range(8)])


def place(d):
    return d ^ (d >> 1)


def rotated(u, cosine, sine):
    return u * cosine + pltpu.roll(u, HD // 2, 1) * sine


def project_kernel(
    scal, x0, f1, b1, f2, b2, f3, b3, f4, b4, gain, cosine, sine, wq, wkv, q_out, n_out
):
    z = scal[Z_AT]
    last = jnp.concatenate([f4[...], b4[...]], axis=0)
    chunks = [r[...].astype(jnp.float32) for r in (x0, f1, b1, f2, b2, f3, b3)]
    chunks.append(last.astype(jnp.float32))
    squares = chunks[0] * chunks[0]
    for chunk in chunks[1:]:
        squares = squares + chunk * chunk
    mean = jnp.sum(squares, axis=1, keepdims=True) * (1.0 / 4096.0)
    inverse = lax.rsqrt(mean + EPSILON)
    acc_q = jnp.zeros((128, 512), jnp.float32)
    acc_n = jnp.zeros((128, 256), jnp.float32)
    for i, shift in enumerate((0, 1, 7, 2, 6, 3, 5, 4)):
        src = (z + 8 - shift) % 8
        rows = pl.ds(pl.multiple_of(src * 512, 512), 512)
        normed = (chunks[i] * inverse * gain[pl.ds(src, 1), 0, :]).astype(jnp.bfloat16)
        acc_q = acc_q + jnp.dot(normed, wq[rows, :], preferred_element_type=jnp.float32)
        acc_n = acc_n + jnp.dot(normed, wkv[rows, :], preferred_element_type=jnp.float32)
    cos = cosine[...]
    sin = sine[...]
    for h in range(4):
        part = rotated(acc_q[:, h * HD : (h + 1) * HD], cos, sin)
        q_out[h * 128 : (h + 1) * 128, :] = part.astype(jnp.bfloat16)
    n_out[:, :HD] = rotated(acc_n[:, :HD], cos, sin).astype(jnp.bfloat16)
    n_out[:, HD:] = acc_n[:, HD:].astype(jnp.bfloat16)


def project(scal, chunks, gain, cosine, sine, w_query, w_keyval):
    return pl.pallas_call(
        project_kernel,
        out_shape=(
            jax.ShapeDtypeStruct((512, HD), jnp.bfloat16),
            jax.ShapeDtypeStruct((128, 256), jnp.bfloat16),
        ),
        grid_spec=pltpu.PrefetchScalarGridSpec(
            num_scalar_prefetch=1,
            grid=(),
            in_specs=[VM] * 14,
            out_specs=(VM, VM),
        ),
        compiler_params=pltpu.CompilerParams(vmem_limit_bytes=PROJECT_VMEM),
        cost_estimate=pl.CostEstimate(
            flops=2 * 128 * 4096 * 768, bytes_accessed=8 << 20, transcendentals=0
        ),
        name="project",
    )(scal, *chunks, gain, cosine, sine, w_query, w_keyval)


def soften(scores, values, m, l, acc):
    top = jnp.maximum(m, jnp.max(scores, axis=0, keepdims=True))
    weights = jnp.exp2((scores - top) * SCALE2)
    factor = jnp.exp2((m - top) * SCALE2)
    total = l * factor + jnp.sum(weights, axis=0, keepdims=True)
    mixed = lax.dot_general(
        values,
        weights.astype(jnp.bfloat16),
        (((0,), (0,)), ((), ())),
        preferred_element_type=jnp.float32,
    )
    return top, total, acc * factor + mixed


def against(keys, q):
    return lax.dot_general(keys, q, (((1,), (1,)), ((), ())), preferred_element_type=jnp.float32)


def cached_kernel(scal, q, *rest):
    refs = rest[:10]
    m_ref, l_ref, acc, kv, sem = rest[10:]
    length = scal[LEN_AT + scal[S_AT] // NEW]
    cached = (length + BLOCK - 1) // BLOCK
    n = 0
    for ref in refs:
        for i in range(ref.shape[0]):
            at = scal[n]
            n += 1

            @pl.when(at >= 0)
            def _(ref=ref, i=i, at=at):
                pltpu.make_async_copy(ref.at[i], kv.at[at], sem.at[at]).start()

    m_ref[...] = jnp.full_like(m_ref, MASKED)
    l_ref[...] = jnp.zeros_like(l_ref)
    acc[...] = jnp.zeros_like(acc)

    def step(first, count, limit=None):
        for b in range(count):
            pltpu.make_async_copy(refs[0].at[0], kv.at[first + b], sem.at[first + b]).wait()
        pages = kv[pl.ds(first, count)].reshape(count * BLOCK, 256)
        scores = against(pages[:, :HD], q[...])
        if limit is not None:
            row = lax.broadcasted_iota(jnp.int32, scores.shape, 0)
            scores = jnp.where(row < limit, scores, MASKED)
        top, total, mixed = soften(scores, pages[:, HD:], m_ref[...], l_ref[...], acc[...])
        m_ref[...] = top
        l_ref[...] = total
        acc[...] = mixed

    whole = length // (8 * BLOCK)

    @pl.loop(0, whole)
    def _(i):
        step(i * 8, 8)

    @pl.loop(whole * 8, cached)
    def _(j):
        step(j, 1, length - j * BLOCK)


def attend_cached(scal, q, buffers):
    return pl.pallas_call(
        cached_kernel,
        out_shape=(
            jax.ShapeDtypeStruct((1, 512), jnp.float32),
            jax.ShapeDtypeStruct((1, 512), jnp.float32),
            jax.ShapeDtypeStruct((128, 512), jnp.float32),
        ),
        grid_spec=pltpu.PrefetchScalarGridSpec(
            num_scalar_prefetch=1,
            grid=(),
            in_specs=[VM] + [ANY] * 10,
            out_specs=(VM, VM, VM),
            scratch_shapes=[
                pltpu.VMEM((CACHED, BLOCK, 256), jnp.bfloat16),
                pltpu.SemaphoreType.DMA((CACHED,)),
            ],
        ),
        compiler_params=pltpu.CompilerParams(vmem_limit_bytes=ATTEND_VMEM),
        cost_estimate=pl.CostEstimate(
            flops=4 * 512 * 128 * 4096, bytes_accessed=4 << 20, transcendentals=512 * 4096
        ),
        name="attend_cached",
    )(scal, q, *buffers)


def fresh_kernel(scal, q, m_in, l_in, acc_in, fa, fb, out):
    me = scal[S_AT]
    core, my_x, my_y = me % 2, (me // 2) % 4, me // 8
    mine = me % NEW
    row = lax.broadcasted_iota(jnp.int32, (BLOCK, 512), 0)
    column = lax.broadcasted_iota(jnp.int32, (BLOCK, 512), 1)
    ahead = (column & 127) - row
    m, l, acc = m_in[...], l_in[...], acc_in[...]
    for ref, c in ((fa, core), (fb, 1 - core)):
        pages = ref[...].reshape(8 * BLOCK, 256)
        scores = against(pages[:, :HD], q[...])
        parts = []
        for i in range(8):
            x = (my_x - (0, 1, 3, 2)[i // 2]) & 3
            y = (my_y ^ (i % 2)) & 1
            block = (y * 4 + x) * 2 + c
            part = scores[i * BLOCK : (i + 1) * BLOCK, :]
            parts.append(jnp.where(ahead >= (block - mine) * BLOCK, part, MASKED))
        scores = jnp.concatenate(parts, axis=0)
        m, l, acc = soften(scores, pages[:, HD:], m, l, acc)
    for h in range(4):
        columns = slice(h * HD, (h + 1) * HD)
        out[:, columns] = (acc[:, columns] / l[:, columns]).T.astype(jnp.bfloat16)


def attend_fresh(scal, q, state, fresh_own, fresh_other):
    return pl.pallas_call(
        fresh_kernel,
        out_shape=jax.ShapeDtypeStruct((128, 512), jnp.bfloat16),
        grid_spec=pltpu.PrefetchScalarGridSpec(
            num_scalar_prefetch=1, grid=(), in_specs=[VM] * 6, out_specs=VM
        ),
        compiler_params=pltpu.CompilerParams(vmem_limit_bytes=ATTEND_VMEM),
        cost_estimate=pl.CostEstimate(
            flops=4 * 512 * 128 * 2048, bytes_accessed=2 << 20, transcendentals=512 * 2048
        ),
        name="attend_fresh",
    )(scal, q, *state, fresh_own, fresh_other)


def output_kernel(shifts, scal, attended, w_out, *outs):
    z = scal[Z_AT]
    rows = attended[...]
    n = 0
    for shift in shifts:
        to = (z + shift) % 8
        columns = pl.ds(pl.multiple_of(to * 512, 512), 512)
        term = jnp.dot(rows, w_out[:, columns], preferred_element_type=jnp.float32)
        if shift == 4:
            outs[n][...] = term[:64].astype(jnp.bfloat16)
            outs[n + 1][...] = term[64:].astype(jnp.bfloat16)
            n += 2
        else:
            outs[n][...] = term.astype(outs[n].dtype)
            n += 1


def output_terms(scal, attended, w_out, shifts):
    shapes = []
    for k in shifts:
        if k == 4:
            shapes += [jax.ShapeDtypeStruct((64, 512), jnp.bfloat16)] * 2
        else:
            kind = jnp.float32 if k == 0 else jnp.bfloat16
            shapes.append(jax.ShapeDtypeStruct((128, 512), kind))
    n = len(shifts)
    return pl.pallas_call(
        functools.partial(output_kernel, shifts),
        out_shape=shapes,
        grid_spec=pltpu.PrefetchScalarGridSpec(
            num_scalar_prefetch=1, grid=(), in_specs=[VM] * 2, out_specs=[VM] * len(shapes)
        ),
        compiler_params=pltpu.CompilerParams(vmem_limit_bytes=SMALL_VMEM),
        cost_estimate=pl.CostEstimate(
            flops=2 * 128 * 512 * 512 * n, bytes_accessed=n << 19, transcendentals=0
        ),
        name="output_terms",
    )(scal, attended, w_out)


def sum_kernel(t_up, t_down, up, down, up_out, down_out):
    for term, moved, out, at in ((t_up, up, up_out, 0), (t_down, down, down_out, 64)):
        n = moved.shape[0]
        at = at if n == 64 else 0
        if n == 64:
            out[...] = term[...]
        both = term[at : at + n, :].astype(jnp.float32) + moved[...].astype(jnp.float32)
        out[at : at + n, :] = both.astype(jnp.bfloat16)


def sums(t_up, t_down, up, down):
    return pl.pallas_call(
        sum_kernel,
        out_shape=[jax.ShapeDtypeStruct((128, 512), jnp.bfloat16)] * 2,
        in_specs=[VM] * 4,
        out_specs=[VM] * 2,
        compiler_params=pltpu.CompilerParams(vmem_limit_bytes=SMALL_VMEM),
        cost_estimate=pl.CostEstimate(flops=1 << 17, bytes_accessed=3 << 18, transcendentals=0),
        name="sums",
    )(t_up, t_down, up, down)


def write_kernel(scal, cache, fa, fb, ga, gb, out, buf, sem):
    me = scal[S_AT]
    core, my_x, my_y = me % 2, (me // 2) % 4, me // 8
    base = me * 3
    found = [jnp.int32(0)] * 3
    for entry in range(96):
        slot = scal[BT_AT + entry] - base
        for i in range(3):
            found[i] = jnp.where(slot == i, entry, found[i])
    starts = []
    for i in range(3):
        request = found[i] // MAXBLK
        start = (found[i] % MAXBLK) * BLOCK - scal[LEN_AT + request]
        block = (start + 64 * BLOCK) // BLOCK - 64
        starts.append((start, block))
        for half in range(2):
            k = block + half
            inside = (k >= 0) & (k < NEW)
            safe = jnp.clip(k, 0, NEW - 1)
            device = request * NEW + safe
            c, x, y = device % 2, (device // 2) % 4, device // 8
            index = 2 * place((my_x - x) & 3) + ((my_y ^ y) & 1)
            near = (y // 2) == (my_y // 2)
            same = c == core
            for cond, ref in (
                (near & same, fa),
                (near & jnp.logical_not(same), fb),
                (jnp.logical_not(near) & same, ga),
                (jnp.logical_not(near) & jnp.logical_not(same), gb),
            ):

                @pl.when(cond & inside)
                def _(ref=ref, index=index, n=2 * i + half):
                    pltpu.make_async_copy(ref.at[index], buf.at[n], sem.at[n]).start()

            @pl.when(jnp.logical_not(inside))
            def _(n=2 * i + half):
                buf[n] = jnp.zeros((BLOCK, 256), jnp.bfloat16)

    row = lax.broadcasted_iota(jnp.int32, (BLOCK, BLOCK), 0)
    column = lax.broadcasted_iota(jnp.int32, (BLOCK, BLOCK), 1)
    tall = lax.broadcasted_iota(jnp.int32, (BLOCK, 256), 0)
    for i in range(3):
        start, block = starts[i]
        offset = start - block * BLOCK
        for half in range(2):
            k = block + half

            @pl.when((k >= 0) & (k < NEW))
            def _(n=2 * i + half):
                pltpu.make_async_copy(fa.at[0], buf.at[n], sem.at[n]).wait()

        low = jnp.where(column == row + offset, 1.0, 0.0).astype(jnp.bfloat16)
        high = jnp.where(column + BLOCK == row + offset, 1.0, 0.0).astype(jnp.bfloat16)
        rows = jnp.dot(low, buf[2 * i], preferred_element_type=jnp.float32)
        rows = rows + jnp.dot(high, buf[2 * i + 1], preferred_element_type=jnp.float32)
        token = tall + start
        written = (token >= 0) & (token < NEW * BLOCK)
        out[i] = jnp.where(written, rows, cache[i].astype(jnp.float32)).astype(jnp.bfloat16)


def write_rows(scal, kv_cache, *fresh):
    return pl.pallas_call(
        write_kernel,
        out_shape=jax.ShapeDtypeStruct(kv_cache.shape, jnp.bfloat16),
        grid_spec=pltpu.PrefetchScalarGridSpec(
            num_scalar_prefetch=1,
            grid=(),
            in_specs=[VM] + [ANY] * 4,
            out_specs=VM,
            scratch_shapes=[
                pltpu.VMEM((6, BLOCK, 256), jnp.bfloat16),
                pltpu.SemaphoreType.DMA((6,)),
            ],
        ),
        compiler_params=pltpu.CompilerParams(vmem_limit_bytes=SMALL_VMEM),
        cost_estimate=pl.CostEstimate(
            flops=2 * 3 * 128 * 256 * 256, bytes_accessed=1 << 20, transcendentals=0
        ),
        name="write_rows",
    )(scal, kv_cache, *fresh)


def cache_places(s, cached_lengths, block_table):
    core, my_x, my_y = s % 2, (s // 2) % 4, s // 8
    entry = np.arange(96)
    other = entry // 48
    far = np.array([0, 1, 3, 2])[entry % 48 // 12]
    near = np.array([0, 1, 3, 2])[entry % 12 // 3]
    c = core ^ other
    x = (my_x - jnp.where(c == 0, near, far)) & 3
    y = (my_y - jnp.where(c == 0, far, near)) & 3
    slot = ((y * 4 + x) * 2 + c) * 3 + entry % 3
    logical = np.arange(96, dtype=np.int32)
    request = logical // MAXBLK
    length = jnp.where(request == 0, cached_lengths[0], cached_lengths[1])
    wanted = (request == s // NEW) & (logical % MAXBLK * BLOCK < length)
    match = (block_table[None, :] == slot[:, None]) & wanted[None, :]
    return jnp.sum(jnp.where(match, logical % MAXBLK + 1, 0), axis=1) - 1


def shards(hidden_in, norm_gain, w_query, w_keyval, w_out, kv_cache, cached_lengths, block_table):
    s = lax.axis_index("seq")
    z = lax.axis_index("tp")
    places = cache_places(s, cached_lengths, block_table)
    scal = jnp.concatenate(
        [places, block_table, cached_lengths, jnp.stack([s, z]).astype(jnp.int32)]
    )
    length = jnp.where(s < NEW, cached_lengths[0], cached_lengths[1])
    position = length + (s % NEW) * BLOCK + jnp.arange(BLOCK, dtype=jnp.int32)
    frequency = ROPE_BASE ** (-2.0 * (np.arange(HD) % (HD // 2)) / HD)
    angles = position.astype(jnp.float32)[:, None] * frequency.astype(np.float32)[None, :]
    cosine = jnp.cos(angles)
    sine = jnp.sin(angles) * np.where(np.arange(HD) < HD // 2, -1.0, 1.0).astype(np.float32)
    gain = norm_gain.astype(jnp.float32).reshape(8, 1, 512)

    up, down = [hidden_in], [hidden_in]
    for _ in range(3):
        up.append(move_z(up[-1], 1))
        down.append(move_z(down[-1], -1))
    up.append(move_z(up[3][:64], 1))
    down.append(move_z(down[3][64:], -1))
    chunks = [hidden_in] + [a for k in range(1, 5) for a in (up[k], down[k])]

    own = kv_cache.reshape(384, 256)
    near = jnp.concatenate(
        [
            own,
            first_axis(own, 1),
            first_axis(own, -1),
            first_axis(own[:192], 2),
            first_axis(own[192:], -2),
        ],
        axis=0,
    ).reshape(12, BLOCK, 256)
    own_set = [
        near,
        second_axis(near, 1),
        second_axis(near, -1),
        second_axis(near[:6], 2),
        second_axis(near[6:], -2),
    ]
    other_set = [other_core(a) for a in own_set]

    queries, fresh = project(scal, chunks, gain, cosine, sine, w_query, w_keyval)
    two = jnp.stack([fresh, pair_y(fresh)])
    fresh_own = jnp.concatenate(
        [two, move_x(two, 1), move_x(two, -1), move_x(two[:1], 2), move_x(two[1:], -2)], axis=0
    )
    fresh_other = other_core(fresh_own)
    state = attend_cached(scal, queries, own_set + other_set)
    attended = attend_fresh(scal, queries, state, fresh_own, fresh_other)

    far_own = move_y(fresh_own, 2)
    far_other = other_core(far_own)
    kv_out = write_rows(scal, kv_cache, fresh_own, fresh_other, far_own, far_other)

    t4a, t4b = output_terms(scal, attended, w_out, (4,))
    ahead, behind = move_z(t4a, 1), move_z(t4b, -1)
    t3, t5, t2, t6, t1, t7, t0 = output_terms(scal, attended, w_out, (3, 5, 2, 6, 1, 7, 0))
    for t_up, t_down in ((t3, t5), (t2, t6), (t1, t7)):
        ahead, behind = sums(t_up, t_down, ahead, behind)
        ahead, behind = move_z(ahead, 1), move_z(behind, -1)
    total = t0 + ahead.astype(jnp.float32) + behind.astype(jnp.float32)
    hidden_out = (hidden_in.astype(jnp.float32) + total).astype(jnp.bfloat16)
    return hidden_out, kv_out


def solution(mesh):
    return jax.shard_map(
        shards,
        mesh=mesh,
        in_specs=(
            P("seq", "tp"),
            P(),
            P(None, "tp"),
            P(None, "tp"),
            P("tp", None),
            P("seq", None, "tp"),
            P(),
            P(),
        ),
        out_specs=(P("seq", "tp"), P("seq", None, "tp")),
        check_vma=False,
    )
```

```python
import functools
import math

import jax
import jax.numpy as jnp
import numpy as np
from jax import lax
from jax.experimental import pallas as pl
from jax.experimental.pallas import tpu as pltpu
from jax.sharding import PartitionSpec as P

HD = 128
BLOCK = 128
NEW = 16
MAXBLK = 48
CACHED = 32
EPSILON = 1e-05
ROPE_BASE = 500000.0
MASKED = -1e30
SCALE = 1.0 / math.sqrt(HD)
SCALE2 = SCALE * 1.4426950408889634
PROJECT_VMEM = 4 << 20
ATTEND_VMEM = 20 << 20
SMALL_VMEM = 4 << 20


ANY = pl.BlockSpec(memory_space=pl.ANY)
VM = pl.BlockSpec(memory_space=pltpu.VMEM)


def coords(s):
    return s % 2, (s // 2) % 4, s // 8


def seq_move(value, target):
    pairs = []
    for s in range(32):
        c, x, y = coords(s)
        c2, x2, y2 = target(c, x, y)
        pairs.append((s, ((y2 % 4) * 4 + x2 % 4) * 2 + c2))
    return lax.ppermute(value, "seq", pairs)


def move_x(value, k):
    return seq_move(value, lambda c, x, y: (c, x + k, y))


def move_y(value, k):
    return seq_move(value, lambda c, x, y: (c, x, y + k))


def pair_y(value):
    return seq_move(value, lambda c, x, y: (c, x, y ^ 1))


def other_core(value):
    return seq_move(value, lambda c, x, y: (1 - c, x, y))


def first_axis(value, k):
    return seq_move(value, lambda c, x, y: (c, x + k, y) if c == 0 else (c, x, y + k))


def second_axis(value, k):
    return seq_move(value, lambda c, x, y: (c, x, y + k) if c == 0 else (c, x + k, y))


def move_z(value, k):
    return lax.ppermute(value, "tp", [(i, (i + k) % 8) for i in range(8)])


def place(d):
    return d ^ (d >> 1)


def rotated(u, cosine, sine):
    return u * cosine + pltpu.roll(u, HD // 2, 1) * sine


def project_kernel(
    x0, f1, b1, f2, b2, f3, b3, f4, gain, cosine, sine, wq, wkv, q_out, n_out
):
    z = lax.axis_index("tp")
    chunks = [r[...].astype(jnp.float32) for r in (x0, f1, b1, f2, b2, f3, b3, f4)]
    squares = chunks[0] * chunks[0]
    for chunk in chunks[1:]:
        squares = squares + chunk * chunk
    mean = jnp.sum(squares, axis=1, keepdims=True) * (1.0 / 4096.0)
    inverse = lax.rsqrt(mean + EPSILON)
    acc_q = jnp.zeros((128, 512), jnp.float32)
    acc_n = jnp.zeros((128, 256), jnp.float32)
    for i, shift in enumerate((0, 1, 7, 2, 6, 3, 5, 4)):
        src = (z + 8 - shift) & 7
        rows = pl.ds(pl.multiple_of(src * 512, 512), 512)
        normed = (chunks[i] * inverse * gain[pl.ds(src, 1), 0, :]).astype(jnp.bfloat16)
        acc_q = acc_q + jnp.dot(normed, wq[rows, :], preferred_element_type=jnp.float32)
        acc_n = acc_n + jnp.dot(normed, wkv[rows, :], preferred_element_type=jnp.float32)
    cos = cosine[...]
    sin = sine[...]
    for h in range(4):
        part = rotated(acc_q[:, h * HD : (h + 1) * HD], cos, sin)
        q_out[h * 128 : (h + 1) * 128, :] = part.astype(jnp.bfloat16)
    n_out[:, :HD] = rotated(acc_n[:, :HD], cos, sin).astype(jnp.bfloat16)
    n_out[:, HD:] = acc_n[:, HD:].astype(jnp.bfloat16)


def project(chunks, gain, cosine, sine, w_query, w_keyval):
    return pl.pallas_call(
        project_kernel,
        out_shape=(
            jax.ShapeDtypeStruct((512, HD), jnp.bfloat16),
            jax.ShapeDtypeStruct((128, 256), jnp.bfloat16),
        ),
        in_specs=[VM] * 13,
        out_specs=(VM, VM),
        compiler_params=pltpu.CompilerParams(vmem_limit_bytes=PROJECT_VMEM),
        cost_estimate=pl.CostEstimate(
            flops=2 * 128 * 4096 * 768, bytes_accessed=8 << 20, transcendentals=0
        ),
        name="project",
    )(*chunks, gain, cosine, sine, w_query, w_keyval)


def pack_kernel(own, r1, l1, o1, out):
    for i, ref in enumerate((own, r1, l1, o1)):
        out[3 * i : 3 * i + 3] = ref[...]


def pack(parts):
    return pl.pallas_call(
        pack_kernel,
        out_shape=jax.ShapeDtypeStruct((12, BLOCK, 256), jnp.bfloat16),
        in_specs=[VM] * 4,
        out_specs=VM,
        compiler_params=pltpu.CompilerParams(vmem_limit_bytes=SMALL_VMEM),
        cost_estimate=pl.CostEstimate(flops=0, bytes_accessed=3 << 19, transcendentals=0),
        name="pack",
    )(*parts)


def load_kernel(lengths, frequency, wq, _, wq_out, angles, sem):
    copy = pltpu.make_async_copy(wq, wq_out, sem)
    copy.start()
    me = lax.axis_index("seq")
    first = lengths[me >> 4] + (me & 15) * BLOCK
    position = first + lax.broadcasted_iota(jnp.int32, (BLOCK, HD), 0)
    angles[...] = position.astype(jnp.float32) * frequency[...]
    copy.wait()


def load(cached_lengths, frequency, w_query, gate):
    return pl.pallas_call(
        load_kernel,
        out_shape=(
            jax.ShapeDtypeStruct(w_query.shape, jnp.bfloat16),
            jax.ShapeDtypeStruct((BLOCK, HD), jnp.float32),
        ),
        grid_spec=pltpu.PrefetchScalarGridSpec(
            num_scalar_prefetch=1,
            grid=(),
            in_specs=[VM, pl.BlockSpec(memory_space=pltpu.HBM), ANY],
            out_specs=(VM, VM),
            scratch_shapes=[pltpu.SemaphoreType.DMA],
        ),
        compiler_params=pltpu.CompilerParams(vmem_limit_bytes=SMALL_VMEM),
        cost_estimate=pl.CostEstimate(flops=0, bytes_accessed=4 << 20, transcendentals=0),
        name="load",
    )(cached_lengths, frequency, w_query, gate)


def soften(scores, values, m, l, acc):
    top = jnp.maximum(m, jnp.max(scores, axis=0, keepdims=True))
    weights = jnp.exp2((scores - top) * SCALE2)
    factor = jnp.exp2((m - top) * SCALE2)
    total = l * factor + jnp.sum(weights, axis=0, keepdims=True)
    mixed = lax.dot_general(
        values,
        weights.astype(jnp.bfloat16),
        (((0,), (0,)), ((), ())),
        preferred_element_type=jnp.float32,
    )
    return top, total, acc * factor + mixed


def against(keys, q):
    return lax.dot_general(keys, q, (((1,), (1,)), ((), ())), preferred_element_type=jnp.float32)


def cached_kernel(table, lengths, q, *rest):
    refs = rest[:8]
    m_ref, l_ref, acc, kv, sem, owner = rest[8:]
    me = lax.axis_index("seq")
    core, my_x, my_y = me & 1, (me >> 1) & 3, me >> 3
    request = me >> 4
    length = lengths[request]
    cached = (length + BLOCK - 1) >> 7
    for slot in range(96):
        owner[slot] = -1
    for j in range(CACHED):
        slot = table[request * MAXBLK + j]
        owner[jnp.where(j < cached, slot, 96)] = j
    for n, ref in enumerate(refs):
        far = (0, 1, 3, 2)[n % 4]
        c = core ^ (n // 4)
        for p, near in enumerate((0, 1, 3, 2)):
            x = (my_x - jnp.where(c == 0, near, far)) & 3
            y = (my_y - jnp.where(c == 0, far, near)) & 3
            slot = ((y * 4 + x) * 2 + c) * 3
            for i in range(3):
                at = owner[slot + i]

                @pl.when(at >= 0)
                def _(ref=ref, row=3 * p + i, at=at):
                    pltpu.make_async_copy(ref.at[row], kv.at[at], sem.at[at]).start()

    m_ref[...] = jnp.full_like(m_ref, MASKED)
    l_ref[...] = jnp.zeros_like(l_ref)
    acc[...] = jnp.zeros_like(acc)

    def step(first, count, limit=None):
        for b in range(count):
            pltpu.make_async_copy(refs[0].at[0], kv.at[first + b], sem.at[first + b]).wait()
        pages = kv[pl.ds(first, count)].reshape(count * BLOCK, 256)
        scores = against(pages[:, :HD], q[...])
        if limit is not None:
            row = lax.broadcasted_iota(jnp.int32, scores.shape, 0)
            scores = jnp.where(row < limit, scores, MASKED)
        top, total, mixed = soften(scores, pages[:, HD:], m_ref[...], l_ref[...], acc[...])
        m_ref[...] = top
        l_ref[...] = total
        acc[...] = mixed

    whole = length // (8 * BLOCK)

    @pl.loop(0, whole)
    def _(i):
        step(i * 8, 8)

    @pl.loop(whole * 8, cached)
    def _(j):
        step(j, 1, length - j * BLOCK)


def attend_cached(block_table, cached_lengths, q, buffers):
    return pl.pallas_call(
        cached_kernel,
        out_shape=(
            jax.ShapeDtypeStruct((1, 512), jnp.float32),
            jax.ShapeDtypeStruct((1, 512), jnp.float32),
            jax.ShapeDtypeStruct((128, 512), jnp.float32),
        ),
        grid_spec=pltpu.PrefetchScalarGridSpec(
            num_scalar_prefetch=2,
            grid=(),
            in_specs=[VM] + [ANY] * 8,
            out_specs=(VM, VM, VM),
            scratch_shapes=[
                pltpu.VMEM((CACHED, BLOCK, 256), jnp.bfloat16),
                pltpu.SemaphoreType.DMA((CACHED,)),
                pltpu.SMEM((97,), jnp.int32),
            ],
        ),
        compiler_params=pltpu.CompilerParams(vmem_limit_bytes=ATTEND_VMEM),
        cost_estimate=pl.CostEstimate(
            flops=4 * 512 * 128 * 4096, bytes_accessed=4 << 20, transcendentals=512 * 4096
        ),
        name="attend_cached",
    )(block_table, cached_lengths, q, *buffers)


def fresh_kernel(q, m_in, l_in, acc_in, fa, fb, out):
    me = lax.axis_index("seq")
    core, my_x, my_y = me & 1, (me >> 1) & 3, me >> 3
    mine = me & 15
    row = lax.broadcasted_iota(jnp.int32, (BLOCK, 512), 0)
    column = lax.broadcasted_iota(jnp.int32, (BLOCK, 512), 1)
    ahead = (column & 127) - row
    m, l, acc = m_in[...], l_in[...], acc_in[...]
    for ref, c in ((fa, core), (fb, 1 - core)):
        pages = ref[...].reshape(8 * BLOCK, 256)
        scores = against(pages[:, :HD], q[...])
        parts = []
        for i in range(8):
            x = (my_x - (0, 1, 3, 2)[i // 2]) & 3
            y = (my_y ^ (i % 2)) & 1
            block = (y * 4 + x) * 2 + c
            part = scores[i * BLOCK : (i + 1) * BLOCK, :]
            parts.append(jnp.where(ahead >= (block - mine) * BLOCK, part, MASKED))
        scores = jnp.concatenate(parts, axis=0)
        m, l, acc = soften(scores, pages[:, HD:], m, l, acc)
    for h in range(4):
        columns = slice(h * HD, (h + 1) * HD)
        out[:, columns] = (acc[:, columns] / l[:, columns]).T.astype(jnp.bfloat16)


def attend_fresh(q, state, fresh_own, fresh_other):
    return pl.pallas_call(
        fresh_kernel,
        out_shape=jax.ShapeDtypeStruct((128, 512), jnp.bfloat16),
        in_specs=[VM] * 6,
        out_specs=VM,
        compiler_params=pltpu.CompilerParams(vmem_limit_bytes=ATTEND_VMEM),
        cost_estimate=pl.CostEstimate(
            flops=4 * 512 * 128 * 2048, bytes_accessed=2 << 20, transcendentals=512 * 2048
        ),
        name="attend_fresh",
    )(q, *state, fresh_own, fresh_other)


def output_kernel(shifts, attended, w_out, *outs):
    z = lax.axis_index("tp")
    rows = attended[...]
    for shift, out in zip(shifts, outs):
        to = (z + shift) & 7
        columns = pl.ds(pl.multiple_of(to * 512, 512), 512)
        term = jnp.dot(rows, w_out[:, columns], preferred_element_type=jnp.float32)
        out[...] = term.astype(out.dtype)


def output_terms(attended, w_out, shifts):
    n = len(shifts)
    return pl.pallas_call(
        functools.partial(output_kernel, shifts),
        out_shape=[
            jax.ShapeDtypeStruct((128, 512), jnp.float32 if k == 0 else jnp.bfloat16)
            for k in shifts
        ],
        in_specs=[VM] * 2,
        out_specs=[VM] * n,
        compiler_params=pltpu.CompilerParams(vmem_limit_bytes=SMALL_VMEM),
        cost_estimate=pl.CostEstimate(
            flops=2 * 128 * 512 * 512 * n, bytes_accessed=n << 19, transcendentals=0
        ),
        name="output_terms",
    )(attended, w_out)


def sum_kernel(n, *refs):
    for term, moved, out in zip(refs[:n], refs[n : 2 * n], refs[2 * n :]):
        both = term[...].astype(jnp.float32) + moved[...].astype(jnp.float32)
        out[...] = both.astype(jnp.bfloat16)


def sums(terms, moved):
    n = len(terms)
    return pl.pallas_call(
        functools.partial(sum_kernel, n),
        out_shape=[jax.ShapeDtypeStruct((128, 512), jnp.bfloat16)] * n,
        in_specs=[VM] * (2 * n),
        out_specs=[VM] * n,
        compiler_params=pltpu.CompilerParams(vmem_limit_bytes=SMALL_VMEM),
        cost_estimate=pl.CostEstimate(flops=1 << 17, bytes_accessed=3 << 18, transcendentals=0),
        name="sums",
    )(*terms, *moved)


def write_kernel(table, lengths, cache, fa, fb, ga, gb, out, buf, sem):
    me = lax.axis_index("seq")
    core, my_x, my_y = me & 1, (me >> 1) & 3, me >> 3
    base = me * 3
    found = [jnp.int32(0)] * 3
    for entry in range(96):
        slot = table[entry] - base
        for i in range(3):
            found[i] = jnp.where(slot == i, entry, found[i])
    starts = []
    for i in range(3):
        request = found[i] // MAXBLK
        start = (found[i] % MAXBLK) * BLOCK - lengths[request]
        block = (start + 64 * BLOCK) // BLOCK - 64
        starts.append((start, block))
        for half in range(2):
            k = block + half
            inside = (k >= 0) & (k < NEW)
            safe = jnp.clip(k, 0, NEW - 1)
            device = request * NEW + safe
            c, x, y = device % 2, (device // 2) % 4, device // 8
            near = (y // 2) == (my_y // 2)
            flip = jnp.where(near, 0, 1)
            index = 2 * place((my_x - x) & 3) + ((my_y ^ y ^ flip) & 1)
            same = c == core
            for cond, ref in (
                (near & same, fa),
                (near & jnp.logical_not(same), fb),
                (jnp.logical_not(near) & same, ga),
                (jnp.logical_not(near) & jnp.logical_not(same), gb),
            ):

                @pl.when(cond & inside)
                def _(ref=ref, index=index, n=2 * i + half):
                    pltpu.make_async_copy(ref.at[index], buf.at[n], sem.at[n]).start()

            @pl.when(jnp.logical_not(inside))
            def _(n=2 * i + half):
                buf[n] = jnp.zeros((BLOCK, 256), jnp.bfloat16)

    row = lax.broadcasted_iota(jnp.int32, (BLOCK, BLOCK), 0)
    column = lax.broadcasted_iota(jnp.int32, (BLOCK, BLOCK), 1)
    tall = lax.broadcasted_iota(jnp.int32, (BLOCK, 256), 0)
    for i in range(3):
        start, block = starts[i]
        offset = start - block * BLOCK
        for half in range(2):
            k = block + half

            @pl.when((k >= 0) & (k < NEW))
            def _(n=2 * i + half):
                pltpu.make_async_copy(fa.at[0], buf.at[n], sem.at[n]).wait()

        low = jnp.where(column == row + offset, 1.0, 0.0).astype(jnp.bfloat16)
        high = jnp.where(column + BLOCK == row + offset, 1.0, 0.0).astype(jnp.bfloat16)
        rows = jnp.dot(low, buf[2 * i], preferred_element_type=jnp.float32)
        rows = rows + jnp.dot(high, buf[2 * i + 1], preferred_element_type=jnp.float32)
        token = tall + start
        written = (token >= 0) & (token < NEW * BLOCK)
        out[i] = jnp.where(written, rows, cache[i].astype(jnp.float32)).astype(jnp.bfloat16)


def write_rows(block_table, cached_lengths, kv_cache, *fresh):
    return pl.pallas_call(
        write_kernel,
        out_shape=jax.ShapeDtypeStruct(kv_cache.shape, jnp.bfloat16),
        grid_spec=pltpu.PrefetchScalarGridSpec(
            num_scalar_prefetch=2,
            grid=(),
            in_specs=[VM] + [ANY] * 4,
            out_specs=VM,
            scratch_shapes=[
                pltpu.VMEM((6, BLOCK, 256), jnp.bfloat16),
                pltpu.SemaphoreType.DMA((6,)),
            ],
        ),
        compiler_params=pltpu.CompilerParams(vmem_limit_bytes=SMALL_VMEM),
        cost_estimate=pl.CostEstimate(
            flops=2 * 3 * 128 * 256 * 256, bytes_accessed=1 << 20, transcendentals=0
        ),
        name="write_rows",
    )(block_table, cached_lengths, kv_cache, *fresh)


def after(value, *others):
    return lax.optimization_barrier((value, *others))[0]


def shards(hidden_in, norm_gain, w_query, w_keyval, w_out, kv_cache, cached_lengths, block_table):
    s = lax.axis_index("seq")

    up, down = [hidden_in], [hidden_in]
    for _ in range(3):
        up.append(move_z(up[-1], 1))
        down.append(move_z(down[-1], -1))
    up.append(move_z(up[3], 1))
    chunks = [hidden_in, up[1], down[1], up[2], down[2], up[3], down[3], up[4]]

    frequency = ROPE_BASE ** (-2.0 * (np.arange(HD) % (HD // 2)) / HD)
    frequency = jnp.asarray(frequency.astype(np.float32)[None, :])
    w_query, angles = load(cached_lengths, frequency, w_query, down[1])
    angles = after(angles, down[3])
    cosine = jnp.cos(angles)
    sine = jnp.sin(angles) * np.where(np.arange(HD) < HD // 2, -1.0, 1.0).astype(np.float32)
    gain = after(norm_gain, down[3]).astype(jnp.float32).reshape(8, 1, 512)

    parts = [kv_cache] + [first_axis(kv_cache, k) for k in (1, -1, 2)]
    near = pack(parts)
    own_set = [near] + [second_axis(near, k) for k in (1, -1, 2)]
    other_set = [other_core(a) for a in own_set]

    queries, fresh = project(chunks, gain, cosine, sine, w_query, w_keyval)
    two = jnp.stack([fresh, pair_y(fresh)])
    fresh_own = jnp.concatenate([two] + [move_x(two, k) for k in (1, -1, 2)], axis=0)
    fresh_other = other_core(fresh_own)
    far_own = seq_move(fresh_own, lambda c, x, y: (c, x, 3 - y))
    state = attend_cached(block_table, cached_lengths, queries, own_set + other_set)
    attended = attend_fresh(queries, state, fresh_own, fresh_other)

    t4, t5 = output_terms(attended, w_out, (4, 5))
    ahead, behind = move_z(t4, 1), move_z(t5, -1)
    t3, t6, t2, t7, t1, t0 = output_terms(after(attended, t4), w_out, (3, 6, 2, 7, 1, 0))

    ahead, behind = sums((t3, t6), (ahead, behind))
    ahead, behind = move_z(ahead, 1), move_z(behind, -1)
    ahead, behind = sums((t2, t7), (ahead, behind))
    far_other = other_core(after(far_own, ahead))
    ahead, behind = move_z(ahead, 1), move_z(behind, -1)
    kv_out = write_rows(
        block_table, cached_lengths, kv_cache, fresh_own, fresh_other, far_own, far_other
    )
    (ahead,) = sums((t1,), (ahead,))
    ahead = move_z(ahead, 1)
    t0 = after(t0, kv_out)
    total = t0 + behind.astype(jnp.float32) + ahead.astype(jnp.float32)
    hidden_out = (hidden_in.astype(jnp.float32) + total).astype(jnp.bfloat16)
    return hidden_out, kv_out


def solution(mesh):
    return jax.shard_map(
        shards,
        mesh=mesh,
        in_specs=(
            P("seq", "tp"),
            P(),
            P(None, "tp"),
            P(None, "tp"),
            P("tp", None),
            P("seq", None, "tp"),
            P(),
            P(),
        ),
        out_specs=(P("seq", "tp"), P("seq", None, "tp")),
        check_vma=False,
    )
```

```python
import functools
import math

import jax
import jax.numpy as jnp
import numpy as np
from jax import lax
from jax.experimental import pallas as pl
from jax.experimental.pallas import tpu as pltpu
from jax.sharding import PartitionSpec as P


HD = 128
BLOCK = 128
NEW = 16
MAXBLK = 48
CACHED = 32
EPSILON = 1e-05
ROPE_BASE = 500000.0
MASKED = -1e30
SCALE = 1.0 / math.sqrt(HD)
SCALE2 = SCALE * 1.4426950408889634
PARTS = ((0, 0), (0, 1), (0, 3), (1, 0), (1, 1), (1, 3), (0, 2), (1, 2))
PROJECT_VMEM = 4 << 20
ATTEND_VMEM = 20 << 20
SMALL_VMEM = 4 << 20


ANY = pl.BlockSpec(memory_space=pl.ANY)
VM = pl.BlockSpec(memory_space=pltpu.VMEM)


def coords(s):
    return s % 2, (s // 2) % 4, s // 8


def seq_move(value, target):
    pairs = []
    for s in range(32):
        c, x, y = coords(s)
        c2, x2, y2 = target(c, x, y)
        pairs.append((s, ((y2 % 4) * 4 + x2 % 4) * 2 + c2))
    return lax.ppermute(value, "seq", pairs)


def move_x(value, k):
    return seq_move(value, lambda c, x, y: (c, x + k, y))


def pair_y(value):
    return seq_move(value, lambda c, x, y: (c, x, y ^ 1))


def other_core(value):
    return seq_move(value, lambda c, x, y: (1 - c, x, y))


def first_axis(value, k):
    return seq_move(value, lambda c, x, y: (c, x + k, y) if c == 0 else (c, x, y + k))


def second_axis(value, k):
    return seq_move(value, lambda c, x, y: (c, x, y + k) if c == 0 else (c, x + k, y))


def move_z(value, k):
    return lax.ppermute(value, "tp", [(i, (i + k) % 8) for i in range(8)])


def place(d):
    return d ^ (d >> 1)


def rotated(u, cosine, sine):
    return u * cosine + pltpu.roll(u, HD // 2, 1) * sine


def project_kernel(
    x0, f1, b1, f2, b2, f3, b3, f4, gain, cosine, sine, wq, wkv, q_out, n_out
):
    z = lax.axis_index("tp")
    chunks = [r[...].astype(jnp.float32) for r in (x0, f1, b1, f2, b2, f3, b3, f4)]
    squares = chunks[0] * chunks[0]
    for chunk in chunks[1:]:
        squares = squares + chunk * chunk
    mean = jnp.sum(squares, axis=1, keepdims=True) * (1.0 / 4096.0)
    inverse = lax.rsqrt(mean + EPSILON)
    acc_q = jnp.zeros((128, 512), jnp.float32)
    acc_n = jnp.zeros((128, 256), jnp.float32)
    for i, shift in enumerate((0, 1, 7, 2, 6, 3, 5, 4)):
        src = (z + 8 - shift) & 7
        rows = pl.ds(pl.multiple_of(src * 512, 512), 512)
        normed = (chunks[i] * inverse * gain[pl.ds(src, 1), 0, :]).astype(jnp.bfloat16)
        acc_q = acc_q + jnp.dot(normed, wq[rows, :], preferred_element_type=jnp.float32)
        acc_n = acc_n + jnp.dot(normed, wkv[rows, :], preferred_element_type=jnp.float32)
    cos = cosine[...]
    sin = sine[...]
    for h in range(4):
        part = rotated(acc_q[:, h * HD : (h + 1) * HD], cos, sin)
        q_out[h * 128 : (h + 1) * 128, :] = part.astype(jnp.bfloat16)
    n_out[:, :HD] = rotated(acc_n[:, :HD], cos, sin).astype(jnp.bfloat16)
    n_out[:, HD:] = acc_n[:, HD:].astype(jnp.bfloat16)


def project(chunks, gain, cosine, sine, w_query, w_keyval):
    return pl.pallas_call(
        project_kernel,
        out_shape=(
            jax.ShapeDtypeStruct((512, HD), jnp.bfloat16),
            jax.ShapeDtypeStruct((128, 256), jnp.bfloat16),
        ),
        in_specs=[VM] * 13,
        out_specs=(VM, VM),
        compiler_params=pltpu.CompilerParams(vmem_limit_bytes=PROJECT_VMEM),
        cost_estimate=pl.CostEstimate(
            flops=2 * 128 * 4096 * 768, bytes_accessed=8 << 20, transcendentals=0
        ),
        name="project",
    )(*chunks, gain, cosine, sine, w_query, w_keyval)


def pack_kernel(own, r1, l1, o1, out):
    for i, ref in enumerate((own, r1, l1, o1)):
        out[3 * i : 3 * i + 3] = ref[...]


def pack(parts):
    return pl.pallas_call(
        pack_kernel,
        out_shape=jax.ShapeDtypeStruct((12, BLOCK, 256), jnp.bfloat16),
        in_specs=[VM] * 4,
        out_specs=VM,
        compiler_params=pltpu.CompilerParams(vmem_limit_bytes=SMALL_VMEM),
        cost_estimate=pl.CostEstimate(flops=0, bytes_accessed=3 << 19, transcendentals=0),
        name="pack",
    )(*parts)


def prepare_kernel(table, lengths, frequency, _, angles, flags, owner):
    me = lax.axis_index("seq")
    core, my_x, my_y = me & 1, (me >> 1) & 3, me >> 3
    request = me >> 4
    length = lengths[request]
    first = length + (me & 15) * BLOCK
    position = first + lax.broadcasted_iota(jnp.int32, (BLOCK, HD), 0)
    angles[...] = position.astype(jnp.float32) * frequency[...]
    for slot in range(96):
        owner[slot] = 0
    for j in range(CACHED):
        slot = table[request * MAXBLK + j]
        rows = length - j * BLOCK
        owner[slot] = jnp.where(rows >= BLOCK, 1, jnp.where(rows > 0, 2, 0))
    n = 0
    for other, far in PARTS:
        c = core ^ other
        for near in (0, 1, 3, 2):
            x = (my_x - jnp.where(c == 0, near, far)) & 3
            y = (my_y - jnp.where(c == 0, far, near)) & 3
            slot = ((y * 4 + x) * 2 + c) * 3
            for i in range(3):
                flags[n] = owner[slot + i]
                n += 1


def prepare(block_table, cached_lengths, frequency, gate):
    return pl.pallas_call(
        prepare_kernel,
        out_shape=(
            jax.ShapeDtypeStruct((BLOCK, HD), jnp.float32),
            jax.ShapeDtypeStruct((96,), jnp.int32),
        ),
        grid_spec=pltpu.PrefetchScalarGridSpec(
            num_scalar_prefetch=2,
            grid=(),
            in_specs=[VM, ANY],
            out_specs=(VM, pl.BlockSpec(memory_space=pltpu.SMEM)),
            scratch_shapes=[pltpu.SMEM((96,), jnp.int32)],
        ),
        compiler_params=pltpu.CompilerParams(vmem_limit_bytes=SMALL_VMEM),
        cost_estimate=pl.CostEstimate(flops=1 << 31, bytes_accessed=1 << 20, transcendentals=1 << 20),
        name="prepare",
    )(block_table, cached_lengths, frequency, gate)


def soften(scores, values, m, l, acc):
    top = jnp.maximum(m, jnp.max(scores, axis=0, keepdims=True))
    weights = jnp.exp2((scores - top) * SCALE2)
    factor = jnp.exp2((m - top) * SCALE2)
    total = l * factor + jnp.sum(weights, axis=0, keepdims=True)
    mixed = lax.dot_general(
        values,
        weights.astype(jnp.bfloat16),
        (((0,), (0,)), ((), ())),
        preferred_element_type=jnp.float32,
    )
    return top, total, acc * factor + mixed


def against(keys, q):
    return lax.dot_general(keys, q, (((1,), (1,)), ((), ())), preferred_element_type=jnp.float32)


def cached_kernel(part, flags, lengths, q, *rest):
    count = 6 if part else 4
    refs, rest = rest[:count], rest[count:]
    state = rest[:3] if part else None
    places = [(ref, row) for ref in refs for row in range(ref.shape[0])]
    m_ref, l_ref, acc, kv, sem = rest[-5:]
    length = lengths[lax.axis_index("seq") >> 4]
    full = jnp.int32(0)
    partial = jnp.int32(0)
    for n, (ref, row) in enumerate(places):
        flag = flags[part * 48 + n]

        @pl.when(flag == 1)
        def _(ref=ref, row=row, at=jnp.minimum(full, CACHED - 1)):
            pltpu.make_async_copy(ref.at[row], kv.at[at], sem.at[at]).start()

        @pl.when(flag == 2)
        def _(ref=ref, row=row):
            pltpu.make_async_copy(ref.at[row], kv.at[CACHED], sem.at[CACHED]).start()

        full = full + (flag & 1)
        partial = partial + (flag >> 1)

    if part:
        m_ref[...] = state[0][...]
        l_ref[...] = state[1][...]
        acc[...] = state[2][...]
    else:
        m_ref[...] = jnp.full_like(m_ref, MASKED)
        l_ref[...] = jnp.zeros_like(l_ref)
        acc[...] = jnp.zeros_like(acc)

    def step(first, count, limit=None):
        for b in range(count):
            pltpu.make_async_copy(refs[0].at[0], kv.at[first + b], sem.at[first + b]).wait()
        pages = kv[pl.ds(first, count)].reshape(count * BLOCK, 256)
        scores = against(pages[:, :HD], q[...])
        if limit is not None:
            row = lax.broadcasted_iota(jnp.int32, scores.shape, 0)
            scores = jnp.where(row < limit, scores, MASKED)
        top, total, mixed = soften(scores, pages[:, HD:], m_ref[...], l_ref[...], acc[...])
        m_ref[...] = top
        l_ref[...] = total
        acc[...] = mixed

    @pl.loop(0, full >> 3)
    def _(i):
        step(i * 8, 8)

    for count in (4, 2, 1):

        @pl.when((full & count) > 0)
        def _(count=count):
            step(jnp.minimum(full & (64 - 2 * count), CACHED - count), count)

    @pl.when(partial > 0)
    def _():
        step(CACHED, 1, length & (BLOCK - 1))


def attend_cached(part, flags, cached_lengths, q, buffers, state):
    return pl.pallas_call(
        functools.partial(cached_kernel, part),
        out_shape=(
            jax.ShapeDtypeStruct((1, 512), jnp.float32),
            jax.ShapeDtypeStruct((1, 512), jnp.float32),
            jax.ShapeDtypeStruct((128, 512), jnp.float32),
        ),
        grid_spec=pltpu.PrefetchScalarGridSpec(
            num_scalar_prefetch=2,
            grid=(),
            in_specs=[VM] + [ANY] * len(buffers) + [VM] * len(state),
            out_specs=(VM, VM, VM),
            scratch_shapes=[
                pltpu.VMEM((CACHED + 1, BLOCK, 256), jnp.bfloat16),
                pltpu.SemaphoreType.DMA((CACHED + 1,)),
            ],
        ),
        compiler_params=pltpu.CompilerParams(vmem_limit_bytes=ATTEND_VMEM),
        cost_estimate=pl.CostEstimate(
            flops=4 * 512 * 128 * 2048, bytes_accessed=4 << 20, transcendentals=512 * 2048
        ),
        name="attend_cached",
    )(flags, cached_lengths, q, *buffers, *state)


def fresh_kernel(q, m_in, l_in, acc_in, fa, fb, out):
    me = lax.axis_index("seq")
    core, my_x, my_y = me & 1, (me >> 1) & 3, me >> 3
    mine = me & 15
    row = lax.broadcasted_iota(jnp.int32, (BLOCK, 512), 0)
    column = lax.broadcasted_iota(jnp.int32, (BLOCK, 512), 1)
    ahead = (column & 127) - row
    m, l, acc = m_in[...], l_in[...], acc_in[...]
    for ref, c in ((fa, core), (fb, 1 - core)):
        pages = ref[...].reshape(8 * BLOCK, 256)
        scores = against(pages[:, :HD], q[...])
        parts = []
        for i in range(8):
            x = (my_x - (0, 1, 3, 2)[i // 2]) & 3
            y = (my_y ^ (i % 2)) & 1
            block = (y * 4 + x) * 2 + c
            part = scores[i * BLOCK : (i + 1) * BLOCK, :]
            parts.append(jnp.where(ahead >= (block - mine) * BLOCK, part, MASKED))
        scores = jnp.concatenate(parts, axis=0)
        m, l, acc = soften(scores, pages[:, HD:], m, l, acc)
    for h in range(4):
        columns = slice(h * HD, (h + 1) * HD)
        out[:, columns] = (acc[:, columns] / l[:, columns]).T.astype(jnp.bfloat16)


def attend_fresh(q, state, fresh_own, fresh_other):
    return pl.pallas_call(
        fresh_kernel,
        out_shape=jax.ShapeDtypeStruct((128, 512), jnp.bfloat16),
        in_specs=[VM] * 6,
        out_specs=VM,
        compiler_params=pltpu.CompilerParams(vmem_limit_bytes=ATTEND_VMEM),
        cost_estimate=pl.CostEstimate(
            flops=4 * 512 * 128 * 2048, bytes_accessed=2 << 20, transcendentals=512 * 2048
        ),
        name="attend_fresh",
    )(q, *state, fresh_own, fresh_other)


def output_kernel(shifts, attended, w_out, *outs):
    z = lax.axis_index("tp")
    rows = attended[...]
    for shift, out in zip(shifts, outs):
        to = (z + shift) & 7
        columns = pl.ds(pl.multiple_of(to * 512, 512), 512)
        term = jnp.dot(rows, w_out[:, columns], preferred_element_type=jnp.float32)
        out[...] = term.astype(out.dtype)


def output_terms(attended, w_out, shifts):
    n = len(shifts)
    return pl.pallas_call(
        functools.partial(output_kernel, shifts),
        out_shape=[
            jax.ShapeDtypeStruct((128, 512), jnp.float32 if k == 0 else jnp.bfloat16)
            for k in shifts
        ],
        in_specs=[VM] * 2,
        out_specs=[VM] * n,
        compiler_params=pltpu.CompilerParams(vmem_limit_bytes=SMALL_VMEM),
        cost_estimate=pl.CostEstimate(
            flops=2 * 128 * 512 * 512 * n, bytes_accessed=n << 19, transcendentals=0
        ),
        name="output_terms",
    )(attended, w_out)


def sum_kernel(n, *refs):
    for term, moved, out in zip(refs[:n], refs[n : 2 * n], refs[2 * n :]):
        both = term[...].astype(jnp.float32) + moved[...].astype(jnp.float32)
        out[...] = both.astype(jnp.bfloat16)


def sums(terms, moved):
    n = len(terms)
    return pl.pallas_call(
        functools.partial(sum_kernel, n),
        out_shape=[jax.ShapeDtypeStruct((128, 512), jnp.bfloat16)] * n,
        in_specs=[VM] * (2 * n),
        out_specs=[VM] * n,
        compiler_params=pltpu.CompilerParams(vmem_limit_bytes=SMALL_VMEM),
        cost_estimate=pl.CostEstimate(flops=1 << 17, bytes_accessed=3 << 18, transcendentals=0),
        name="sums",
    )(*terms, *moved)


def write_kernel(table, lengths, cache, fa, fb, ga, gb, out, buf, sem):
    me = lax.axis_index("seq")
    core, my_x, my_y = me & 1, (me >> 1) & 3, me >> 3
    base = me * 3
    found = [jnp.int32(0)] * 3
    for entry in range(96):
        slot = table[entry] - base
        for i in range(3):
            found[i] = jnp.where(slot == i, entry, found[i])
    starts = []
    for i in range(3):
        request = found[i] // MAXBLK
        start = (found[i] % MAXBLK) * BLOCK - lengths[request]
        block = (start + 64 * BLOCK) // BLOCK - 64
        starts.append((start, block))
        for half in range(2):
            k = block + half
            inside = (k >= 0) & (k < NEW)
            safe = jnp.clip(k, 0, NEW - 1)
            device = request * NEW + safe
            c, x, y = device % 2, (device // 2) % 4, device // 8
            near = (y // 2) == (my_y // 2)
            flip = jnp.where(near, 0, 1)
            index = 2 * place((my_x - x) & 3) + ((my_y ^ y ^ flip) & 1)
            same = c == core
            for cond, ref in (
                (near & same, fa),
                (near & jnp.logical_not(same), fb),
                (jnp.logical_not(near) & same, ga),
                (jnp.logical_not(near) & jnp.logical_not(same), gb),
            ):

                @pl.when(cond & inside)
                def _(ref=ref, index=index, n=2 * i + half):
                    pltpu.make_async_copy(ref.at[index], buf.at[n], sem.at[n]).start()

            @pl.when(jnp.logical_not(inside))
            def _(n=2 * i + half):
                buf[n] = jnp.zeros((BLOCK, 256), jnp.bfloat16)

    row = lax.broadcasted_iota(jnp.int32, (BLOCK, BLOCK), 0)
    column = lax.broadcasted_iota(jnp.int32, (BLOCK, BLOCK), 1)
    tall = lax.broadcasted_iota(jnp.int32, (BLOCK, 256), 0)
    for i in range(3):
        start, block = starts[i]
        offset = start - block * BLOCK
        for half in range(2):
            k = block + half

            @pl.when((k >= 0) & (k < NEW))
            def _(n=2 * i + half):
                pltpu.make_async_copy(fa.at[0], buf.at[n], sem.at[n]).wait()

        low = jnp.where(column == row + offset, 1.0, 0.0).astype(jnp.bfloat16)
        high = jnp.where(column + BLOCK == row + offset, 1.0, 0.0).astype(jnp.bfloat16)
        rows = jnp.dot(low, buf[2 * i], preferred_element_type=jnp.float32)
        rows = rows + jnp.dot(high, buf[2 * i + 1], preferred_element_type=jnp.float32)
        token = tall + start
        written = (token >= 0) & (token < NEW * BLOCK)
        out[i] = jnp.where(written, rows, cache[i].astype(jnp.float32)).astype(jnp.bfloat16)


def write_rows(block_table, cached_lengths, kv_cache, *fresh):
    return pl.pallas_call(
        write_kernel,
        out_shape=jax.ShapeDtypeStruct(kv_cache.shape, jnp.bfloat16),
        grid_spec=pltpu.PrefetchScalarGridSpec(
            num_scalar_prefetch=2,
            grid=(),
            in_specs=[VM] + [ANY] * 4,
            out_specs=VM,
            scratch_shapes=[
                pltpu.VMEM((6, BLOCK, 256), jnp.bfloat16),
                pltpu.SemaphoreType.DMA((6,)),
            ],
        ),
        compiler_params=pltpu.CompilerParams(vmem_limit_bytes=SMALL_VMEM),
        cost_estimate=pl.CostEstimate(
            flops=2 * 3 * 128 * 256 * 256, bytes_accessed=1 << 20, transcendentals=0
        ),
        name="write_rows",
    )(block_table, cached_lengths, kv_cache, *fresh)


def after(value, *others):
    return lax.optimization_barrier((value, *others))[0]


def shards(hidden_in, norm_gain, w_query, w_keyval, w_out, kv_cache, cached_lengths, block_table):
    up, down = [hidden_in], [hidden_in]
    for _ in range(3):
        up.append(move_z(up[-1], 1))
        down.append(move_z(down[-1], -1))
    up.append(move_z(up[3], 1))
    chunks = [hidden_in, up[1], down[1], up[2], down[2], up[3], down[3], up[4]]

    frequency = ROPE_BASE ** (-2.0 * (np.arange(HD) % (HD // 2)) / HD)
    frequency = jnp.asarray(frequency.astype(np.float32)[None, :])
    angles, flags = prepare(block_table, cached_lengths, frequency, down[2])
    angles = after(angles, down[3])
    cosine = jnp.cos(angles)
    sine = jnp.sin(angles) * np.where(np.arange(HD) < HD // 2, -1.0, 1.0).astype(np.float32)
    gain = after(norm_gain, down[3]).astype(jnp.float32).reshape(8, 1, 512)

    steps = (1, -1, 2)
    near = pack([kv_cache] + [first_axis(kv_cache, k) for k in steps])
    ahead, behind = second_axis(near, 1), second_axis(near, -1)
    far_up = second_axis(ahead[:6], 1)
    far_down = second_axis(behind[6:], -1)
    near_other = other_core(after(near, cosine))
    first_part = [near, ahead, behind, near_other]
    second_part = [other_core(ahead), other_core(behind), far_up, far_down]
    second_part += [other_core(far_up), other_core(far_down)]

    queries, fresh = project(chunks, gain, cosine, sine, w_query, w_keyval)
    two = jnp.stack([fresh, pair_y(fresh)])
    fresh_own = jnp.concatenate([two] + [move_x(two, k) for k in steps], axis=0)
    fresh_other = other_core(fresh_own)
    far_own = seq_move(fresh_own, lambda c, x, y: (c, x, 3 - y))
    state = attend_cached(0, flags, cached_lengths, queries, first_part, ())
    state = attend_cached(1, flags, cached_lengths, queries, second_part, state)
    attended = attend_fresh(queries, state, fresh_own, fresh_other)

    t4, t5 = output_terms(attended, w_out, (4, 5))
    ahead, behind = move_z(t4, 1), move_z(t5, -1)
    t3, t6, t2, t7, t1, t0 = output_terms(after(attended, t4), w_out, (3, 6, 2, 7, 1, 0))
    ahead, behind = sums((t3, t6), (ahead, behind))
    ahead, behind = move_z(ahead, 1), move_z(behind, -1)
    ahead, behind = sums((t2, t7), (ahead, behind))
    far_other = other_core(after(far_own, ahead))
    ahead, behind = move_z(ahead, 1), move_z(behind, -1)
    kv_out = write_rows(
        block_table, cached_lengths, kv_cache, fresh_own, fresh_other, far_own, far_other
    )
    (ahead,) = sums((t1,), (ahead,))
    ahead = move_z(ahead, 1)
    t0 = after(t0, kv_out)
    total = t0 + behind.astype(jnp.float32) + ahead.astype(jnp.float32)
    hidden_out = (hidden_in.astype(jnp.float32) + total).astype(jnp.bfloat16)
    return hidden_out, kv_out


def solution(mesh):
    return jax.shard_map(
        shards,
        mesh=mesh,
        in_specs=(
            P("seq", "tp"),
            P(),
            P(None, "tp"),
            P(None, "tp"),
            P("tp", None),
            P("seq", None, "tp"),
            P(),
            P(),
        ),
        out_specs=(P("seq", "tp"), P("seq", None, "tp")),
        check_vma=False,
    )
```
